32 devices in a mesh: ra: 8 (over z, y), dec: 4 (over x, core).
Axes of the slice: x: 2, y: 2, z: 4, core: 2. Of those that a mesh axis runs over, the one named last changes fastest.
Arguments:
- exposures: float32 [2, 1280, 3072], P(None, 'dec', 'ra'), may hold values from -6 to 6
- inv_variance: float32 [2, 1280, 3072], P(None, 'dec', 'ra'), may hold values from 0.25 to 4
- pixel_valid: int32 [2, 1280, 3072], P(None, 'dec', 'ra'), may hold values 0 or 1
- correlation: int32 [4, 8, 2], P('dec', 'ra'), may hold values 0 or 1
- pixel_offset: int32 [4, 8, 2, 2], P('dec', 'ra'), may hold values from -3 to 3
- subpixel: float32 [4, 8, 2, 2], P('dec', 'ra'), may hold values from -0.5 to 0.5
- psf_match: bfloat16 [63, 63], replicated, may hold values from -0.09375 to 0.09375
Outputs:
- matched: float32 [768, 2048], P('dec', 'ra')
- weight_map: float32 [768, 2048], P('dec', 'ra')
The draws below stay inside these ranges and needn't reach their ends.
All inputs are finite; a program needn't handle non-finite values. No bound on the sum of `pixel_valid` or of `correlation` on one device may be relied on, other than what follows from the above.
Results may differ from the reference program's by a relative error of at most 0.007.
Values may be sent and summed in bfloat16 or wider, within the bound.
A program may use at most 128 MiB of HBM per device.

```python
import math
import jax
import jax.numpy as jnp
from jax import lax

MARGIN = 64
KERNEL = 63
EPOCHS = 2
HALF = 31
PROWS = 320
PCOLS = 384
STRIPS = 4
TILES = 8
NROWS = 768
NCOLS = 2048
SROWS = 1280
SCOLS = 3072


def with_ends(drawn, own_key, least, high):
    place = [jax.random.randint(jax.random.fold_in(own_key, axis), (), 0, length) for axis, length in enumerate(drawn.shape)]
    longest = drawn.shape.index(max(drawn.shape))
    neighbour = place[:longest] + [(place[longest] + 1) % drawn.shape[longest]] + place[longest + 1:]
    return drawn.at[tuple(place)].set(least).at[tuple(neighbour)].set(high)


def levels(rng, extent, pieces, low, high):
    loudness = 1.0
    for position, shards_of in pieces:
        steps = jax.random.uniform(jax.random.fold_in(jax.random.fold_in(rng, 6), position), (shards_of,), jnp.float32, low / len(pieces), high / len(pieces))
        loudness = loudness * jnp.repeat(jnp.exp(steps), extent[position] // shards_of).reshape((-1,) + (1,) * (len(extent) - 1 - position))
    return loudness


def centred(stream_key, extent, width, bound, shards=(), kind=jnp.bfloat16):
    values = width * jax.random.normal(stream_key, extent, jnp.float32)
    if shards:
        values = values * levels(stream_key, extent, shards, -0.22, 0.18)
    return jnp.clip(values, -bound, bound).astype(kind)


def setup_inputs(seed: int = 0) -> dict:
    arg_keys = jax.random.split(jax.random.key(seed), 8)
    return {
        "exposures": centred(arg_keys[0], (EPOCHS, SROWS, SCOLS), 1.0, 6.0, ((1, 4), (2, 8)), jnp.float32),
        "inv_variance": jnp.clip(jnp.exp(math.log(4.0) - 2.7725887 * jax.random.uniform(arg_keys[1], (EPOCHS, SROWS, SCOLS), jnp.float32) ** levels(arg_keys[1], (EPOCHS, SROWS, SCOLS), ((1, 4), (2, 8)), -0.2, 0.2)), 0.25, 4.0),
        "pixel_valid": with_ends((jax.random.randint(arg_keys[2], (EPOCHS, SROWS, SCOLS), 0, 8) < 7).astype(jnp.int32), jax.random.fold_in(arg_keys[2], 1), 0, 1),
        "correlation": with_ends((jax.random.randint(arg_keys[3], (STRIPS, TILES, EPOCHS), 0, 4) < 3).astype(jnp.int32), jax.random.fold_in(arg_keys[3], 1), 0, 1),
        "pixel_offset": with_ends(jax.random.randint(arg_keys[4], (STRIPS, TILES, EPOCHS, 2), -3, 4), jax.random.fold_in(arg_keys[4], 1), -3, 3).astype(jnp.int32),
        "subpixel": jnp.clip(jax.random.uniform(arg_keys[5], (STRIPS, TILES, EPOCHS, 2), jnp.float32, -0.5, 0.5) * levels(arg_keys[5], (STRIPS, TILES, EPOCHS, 2), ((0, 4), (1, 8)), -0.4, 0.0), -0.5, 0.5),
        "psf_match": centred(arg_keys[6], (KERNEL, KERNEL), (KERNEL * KERNEL) ** -0.5, 0.09375),
    }


HIGHEST_PRECISION = lax.Precision.HIGHEST


def lanczos_matrix(size_count, shift_value):
    row_ids = jnp.arange(size_count, dtype=jnp.int32)[:, None]
    col_ids = jnp.arange(size_count, dtype=jnp.int32)[None, :]
    where_at = (row_ids - col_ids).astype(shift_value.dtype) + shift_value
    kernel_value = jnp.sinc(where_at) * jnp.sinc(where_at / 3.0)
    return jnp.where(jnp.abs(where_at) < 3.0, kernel_value, jnp.zeros_like(kernel_value))


def warp_tile(images, weights, valid_bits, offsets, fractions, covered):
    row_count, col_count = images.shape[1], images.shape[2]
    numerator = jnp.zeros((row_count, col_count), images.dtype)
    denominator = jnp.zeros((row_count, col_count), images.dtype)
    for which_epoch in range(images.shape[0]):
        shifts = offsets[which_epoch].astype(fractions.dtype) + fractions[which_epoch]
        row_map = lanczos_matrix(row_count, shifts[0])
        col_map = lanczos_matrix(col_count, shifts[1])
        masked = weights[which_epoch] * valid_bits[which_epoch].astype(weights.dtype) * covered[which_epoch].astype(weights.dtype)
        stacked = jnp.concatenate([masked * images[which_epoch], masked], axis=1)
        half_done = jnp.dot(row_map, stacked, precision=HIGHEST_PRECISION)
        numerator = numerator + jnp.dot(half_done[:, :col_count], col_map.T, precision=HIGHEST_PRECISION)
        denominator = denominator + jnp.dot(half_done[:, col_count:], col_map.T, precision=HIGHEST_PRECISION)
    return numerator, denominator


def shift_tiles(values, grid_axis, offset_by, wrapping):
    if wrapping:
        return jnp.roll(values, offset_by, axis=grid_axis)
    size_count = values.shape[grid_axis]
    empty_slab = jnp.zeros_like(lax.slice_in_dim(values, 0, 1, axis=grid_axis))
    if offset_by > 0:
        return jnp.concatenate([empty_slab, lax.slice_in_dim(values, 0, size_count - 1, axis=grid_axis)], axis=grid_axis)
    return jnp.concatenate([lax.slice_in_dim(values, 1, size_count, axis=grid_axis), empty_slab], axis=grid_axis)


def place_margins(values, pixel_axis, grid_axis, wrapping):
    inner_size = values.shape[pixel_axis] - 2 * MARGIN
    summed = lax.slice_in_dim(values, MARGIN, MARGIN + inner_size, axis=pixel_axis)
    from_lower = shift_tiles(lax.slice_in_dim(values, MARGIN + inner_size, inner_size + 2 * MARGIN, axis=pixel_axis), grid_axis, 1, wrapping)
    from_upper = shift_tiles(lax.slice_in_dim(values, 0, MARGIN, axis=pixel_axis), grid_axis, -1, wrapping)
    pad_lower = [(0, 0)] * values.ndim
    pad_lower[pixel_axis] = (0, inner_size - MARGIN)
    pad_upper = [(0, 0)] * values.ndim
    pad_upper[pixel_axis] = (inner_size - MARGIN, 0)
    return summed + jnp.pad(from_lower, pad_lower) + jnp.pad(from_upper, pad_upper)


def reference(exposures, inv_variance, pixel_valid, correlation, pixel_offset, subpixel, psf_match):
    tile_count = STRIPS * TILES

    def one_tile(flat_index):
        strip_index = flat_index // TILES
        tile_index = flat_index - strip_index * TILES

        def tile_block(source):
            starts = (jnp.zeros((), jnp.int32), (strip_index * PROWS).astype(jnp.int32), (tile_index * PCOLS).astype(jnp.int32))
            return lax.dynamic_slice(source, starts, (EPOCHS, PROWS, PCOLS))

        return warp_tile(tile_block(exposures), tile_block(inv_variance), tile_block(pixel_valid), pixel_offset[strip_index, tile_index], subpixel[strip_index, tile_index], correlation[strip_index, tile_index])

    numerator, denominator = lax.map(one_tile, jnp.arange(tile_count, dtype=jnp.int32))
    planes = jnp.stack([numerator, denominator]).reshape(2, STRIPS, TILES, PROWS, PCOLS)
    planes = place_margins(planes, 4, 2, True)
    planes = place_margins(planes, 3, 1, False)
    planes = planes.transpose(0, 1, 3, 2, 4).reshape(2, NROWS, NCOLS)
    weight_map = planes[1]
    coadded = (planes[0] / jnp.maximum(planes[1], 1.0)).astype(jnp.bfloat16)
    wrapped = jnp.concatenate([coadded[:, NCOLS - HALF:], coadded, coadded[:, :HALF]], axis=1)
    padded = jnp.pad(wrapped, ((HALF, HALF), (0, 0)))
    matched = lax.conv_general_dilated(padded.astype(jnp.float32)[None, None], psf_match.astype(jnp.float32)[None, None], (1, 1), "VALID", precision=HIGHEST_PRECISION)[0, 0]
    return matched, weight_map
```

```python
import functools

import jax
import jax.numpy as jnp
from jax import lax
from jax.experimental import pallas as pl
from jax.experimental.pallas import tpu as pltpu
from jax.sharding import PartitionSpec as P

MARGIN = 64
HALF = 31
LANES = 128
BAND = 96
GROUP = 16
F32 = jnp.float32
BF16 = jnp.bfloat16
MESH = pl.DeviceIdType.MESH


def dot(a, b):
    return jnp.dot(a, b, preferred_element_type=F32)


def dot_t(a, b):
    return lax.dot_general(a, b, (((1,), (1,)), ((), ())), preferred_element_type=F32)


def sinc(x):
    angle = jnp.pi * x
    safe = jnp.where(angle == 0.0, 1.0, angle)
    return jnp.where(angle == 0.0, 1.0, jnp.sin(safe) / safe)


def lanczos(x):
    return jnp.where(jnp.abs(x) < 3.0, sinc(x) * sinc(x / 3.0), 0.0)


def skewed(row, count, width, shift):
    spread = jnp.broadcast_to(row, (count, row.shape[1]))
    return pltpu.roll(spread, shift, 1, stride=1, stride_axis=0)[:, :width]


def halves(value):
    high = value.astype(BF16)
    return high, (value - high.astype(F32)).astype(BF16)


def signed_lanes(width):
    lane = lax.broadcasted_iota(jnp.int32, (1, width), 1)
    return jnp.where(lane >= width // 2, lane - width, lane).astype(F32)


def kernel(
    dims,
    exp_hbm,
    inv_hbm,
    val_hbm,
    cor_ref,
    off_ref,
    sub_ref,
    psf_ref,
    matched_ref,
    weight_ref,
    exp_ref,
    inv_ref,
    val_ref,
    tile,
    dec_out,
    dec_in,
    ra_out,
    ra_in,
    taps,
    bands,
    coadd,
    shifts,
    load_sem,
    dec_send,
    dec_recv,
    ra_send,
    ra_recv,
):
    epochs, prows, pcols, n_ra, n_dec = dims
    rows, cols = prows - 2 * MARGIN, pcols - 2 * MARGIN
    me_ra, me_dec = lax.axis_index("ra"), lax.axis_index("dec")
    prev_ra, next_ra = lax.rem(me_ra + n_ra - 1, n_ra), lax.rem(me_ra + 1, n_ra)
    has_prev, has_next = me_dec > 0, me_dec < n_dec - 1

    loads = []
    for e in range(epochs):
        for which, (src, dst) in enumerate(
            ((exp_hbm, exp_ref), (inv_hbm, inv_ref), (val_hbm, val_ref))
        ):
            loads.append(pltpu.make_async_copy(src.at[e], dst.at[e], load_sem.at[3 * e + which]))
    for copy in loads:
        copy.start()

    barrier = pltpu.get_barrier_semaphore()
    for peer in (prev_ra, next_ra):
        pl.semaphore_signal(barrier, inc=1, device_id=(peer, me_dec), device_id_type=MESH)

    @pl.when(has_prev)
    def _():
        pl.semaphore_signal(barrier, inc=1, device_id=(me_ra, me_dec - 1), device_id_type=MESH)

    @pl.when(has_next)
    def _():
        pl.semaphore_signal(barrier, inc=1, device_id=(me_ra, me_dec + 1), device_id_type=MESH)

    half = prows // 2
    side = 256
    start = prows - side
    maps = []
    for e in range(epochs):
        lanes = signed_lanes(512)
        shift_r = off_ref[0, 0, e, 0].astype(F32) + sub_ref[0, 0, e, 0]
        shift_c = off_ref[0, 0, e, 1].astype(F32) + sub_ref[0, 0, e, 1]
        row = lanczos(shift_r - lanes)
        col = lanczos(shift_c + lanes)
        top = halves(skewed(row, half, side, 0))
        bottom = halves(skewed(row, half, side, half - start))
        across = halves(skewed(col, pcols, pcols, 0))
        maps.append((top, bottom, across))

    for e in range(epochs):
        for which in range(3):
            loads[3 * e + which].wait()
        top, bottom, across = maps[e]
        masked = inv_ref[e] * val_ref[e].astype(F32) * cor_ref[0, 0, e].astype(F32)
        stacked = jnp.concatenate([(masked * exp_ref[e]).astype(BF16), masked.astype(BF16)], axis=1)
        upper = dot(top[0], stacked[:side]) + dot(top[1], stacked[:side])
        lower = dot(bottom[0], stacked[start:]) + dot(bottom[1], stacked[start:])
        done = jnp.concatenate([upper.astype(BF16), lower.astype(BF16)], axis=0)
        for plane in range(2):
            part = done[:, plane * pcols : (plane + 1) * pcols]
            warped = dot(part, across[0]) + dot(part, across[1])
            if e == 0:
                tile[plane] = warped
            else:
                tile[plane] += warped

    dec_out[0] = tile[:, 0:BAND, :].astype(BF16)
    dec_out[1] = tile[:, prows - BAND : prows, :].astype(BF16)
    pl.semaphore_wait(barrier, 2 + has_prev.astype(jnp.int32) + has_next.astype(jnp.int32))

    def dec_copy(way):
        return pltpu.make_async_remote_copy(
            src_ref=dec_out.at[way],
            dst_ref=dec_in.at[way],
            send_sem=dec_send.at[way],
            recv_sem=dec_recv.at[way],
            device_id=(me_ra, me_dec + (1 if way else -1)),
            device_id_type=MESH,
        )

    @pl.when(has_prev)
    def _():
        dec_copy(0).start()

    @pl.when(has_next)
    def _():
        dec_copy(1).start()

    side_k = psf_ref.shape[0]
    taps[...] = jnp.zeros_like(taps)
    taps[0:side_k, 0 : psf_ref.shape[1]] = psf_ref[...].astype(F32)
    offset = MARGIN - HALF

    def build(k, carry):
        for s in range(GROUP // 2):
            for parity in range(2):
                row = taps[pl.ds(k * GROUP + 2 * s + parity, 1), :]
                bands[
                    k, parity * LANES : (parity + 1) * LANES, s * 2 * LANES : (s + 1) * 2 * LANES
                ] = skewed(row, LANES, 2 * LANES, offset).astype(BF16)
        return carry

    lax.fori_loop(0, bands.shape[0], build, 0)

    @pl.when(has_next)
    def _():
        dec_copy(0).wait_recv()
        tile[:, prows - 2 * MARGIN : prows - 2 * MARGIN + BAND, :] += dec_in[0].astype(F32)

    @pl.when(has_prev)
    def _():
        dec_copy(1).wait_recv()
        tile[:, 2 * MARGIN - BAND : 2 * MARGIN, :] += dec_in[1].astype(F32)

    low = MARGIN - 32
    high = low + rows + 64
    ra_out[0] = tile[:, low:high, 0:LANES].astype(BF16)
    ra_out[1] = tile[:, low:high, pcols - LANES : pcols].astype(BF16)

    def ra_copy(way):
        return pltpu.make_async_remote_copy(
            src_ref=ra_out.at[way],
            dst_ref=ra_in.at[way],
            send_sem=ra_send.at[way],
            recv_sem=ra_recv.at[way],
            device_id=(next_ra if way else prev_ra, me_dec),
            device_id_type=MESH,
        )

    ra_copy(0).start()
    ra_copy(1).start()
    ra_copy(0).wait_recv()
    tile[:, low:high, pcols - LANES : pcols] += ra_in[0].astype(F32)
    ra_copy(1).wait_recv()
    tile[:, low:high, 0:LANES] += ra_in[1].astype(F32)

    weight_ref[...] = tile[1, MARGIN : MARGIN + rows, MARGIN : MARGIN + cols]
    row_id = lax.broadcasted_iota(jnp.int32, (coadd.shape[0], 1), 0) - MARGIN + me_dec * rows
    inside = (row_id >= 0) & (row_id < n_dec * rows)
    coadd[...] = jnp.where(inside, tile[0] / jnp.maximum(tile[1], 1.0), 0.0)
    deep = shifts.shape[1]
    for s in range(GROUP // 2):
        first = offset + 2 * s
        moved = coadd[first : first + deep, :].astype(BF16)
        for block in range(2):
            shifts[block, :, s * 2 * LANES : (s + 1) * 2 * LANES] = moved[
                :, block * LANES : (block + 2) * LANES
            ]

    tall = rows + GROUP
    total = jnp.zeros((2 * tall, 2 * LANES), F32)
    for k in range(bands.shape[0]):
        pieces = shifts[:, k * GROUP : k * GROUP + tall, :].reshape(2 * tall, shifts.shape[2])
        total = total + dot_t(pieces, bands[k])
    for block in range(2):
        even = total[block * tall : block * tall + rows, :LANES]
        odd = total[block * tall : (block + 1) * tall, LANES:][1 : rows + 1]
        matched_ref[:, block * LANES : (block + 1) * LANES] = even + odd

    @pl.when(has_prev)
    def _():
        dec_copy(0).wait_send()

    @pl.when(has_next)
    def _():
        dec_copy(1).wait_send()

    ra_copy(0).wait_send()
    ra_copy(1).wait_send()


def solution(mesh):
    n_ra, n_dec = mesh.shape["ra"], mesh.shape["dec"]

    def shards(exposures, inv_variance, pixel_valid, correlation, pixel_offset, subpixel, psf_match):
        epochs, prows, pcols = exposures.shape
        rows, cols = prows - 2 * MARGIN, pcols - 2 * MARGIN
        groups = -(-psf_match.shape[0] // GROUP)
        deep = rows + GROUP * groups
        result = jax.ShapeDtypeStruct((rows, cols), F32)
        hbm = pl.BlockSpec(memory_space=pl.ANY)
        smem = pl.BlockSpec(memory_space=pltpu.SMEM)
        vmem = pl.BlockSpec(memory_space=pltpu.VMEM)
        return pl.pallas_call(
            functools.partial(kernel, (epochs, prows, pcols, n_ra, n_dec)),
            out_shape=(result, result),
            in_specs=[hbm, hbm, hbm, smem, smem, smem, vmem],
            out_specs=(vmem, vmem),
            scratch_shapes=[
                pltpu.VMEM((epochs, prows, pcols), F32),
                pltpu.VMEM((epochs, prows, pcols), F32),
                pltpu.VMEM((epochs, prows, pcols), jnp.int32),
                pltpu.VMEM((2, prows, pcols), F32),
                pltpu.VMEM((2, 2, BAND, pcols), BF16),
                pltpu.VMEM((2, 2, BAND, pcols), BF16),
                pltpu.VMEM((2, 2, rows + 64, LANES), BF16),
                pltpu.VMEM((2, 2, rows + 64, LANES), BF16),
                pltpu.VMEM((groups * GROUP, 2 * LANES), F32),
                pltpu.VMEM((groups, 2 * LANES, GROUP * LANES), BF16),
                pltpu.VMEM((prows, pcols), F32),
                pltpu.VMEM((2, deep, GROUP * LANES), BF16),
                pltpu.SemaphoreType.DMA((3 * epochs,)),
                pltpu.SemaphoreType.DMA((2,)),
                pltpu.SemaphoreType.DMA((2,)),
                pltpu.SemaphoreType.DMA((2,)),
                pltpu.SemaphoreType.DMA((2,)),
            ],
            compiler_params=pltpu.CompilerParams(
                collective_id=0, has_side_effects=True, vmem_limit_bytes=48 * 1024 * 1024
            ),
            name="coadd",
        )(exposures, inv_variance, pixel_valid, correlation, pixel_offset, subpixel, psf_match)

    return jax.shard_map(
        shards,
        mesh=mesh,
        in_specs=(
            P(None, "dec", "ra"),
            P(None, "dec", "ra"),
            P(None, "dec", "ra"),
            P("dec", "ra", None),
            P("dec", "ra", None, None),
            P("dec", "ra", None, None),
            P(),
        ),
        out_specs=(P("dec", "ra"), P("dec", "ra")),
        check_vma=False,
    )
```

```python
import functools

import jax
import jax.numpy as jnp
from jax import lax
from jax.experimental import pallas as pl
from jax.experimental.pallas import tpu as pltpu
from jax.sharding import PartitionSpec as P

MARGIN = 64
HALF = 31
LANES = 128
BAND = 96
GROUP = 16
F32 = jnp.float32
BF16 = jnp.bfloat16
MESH = pl.DeviceIdType.MESH


def dot(a, b):
    return jnp.dot(a, b, preferred_element_type=F32)


def dot_t(a, b):
    return lax.dot_general(a, b, (((1,), (1,)), ((), ())), preferred_element_type=F32)


def sinc(x):
    angle = jnp.pi * x
    safe = jnp.where(angle == 0.0, 1.0, angle)
    return jnp.where(angle == 0.0, 1.0, jnp.sin(safe) / safe)


def lanczos(x):
    return jnp.where(jnp.abs(x) < 3.0, sinc(x) * sinc(x / 3.0), 0.0)


def skewed(row, count, width, shift):
    spread = jnp.broadcast_to(row, (count, row.shape[1]))
    return pltpu.roll(spread, shift, 1, stride=1, stride_axis=0)[:, :width]


def halves(value):
    high = value.astype(BF16)
    return high, (value - high.astype(F32)).astype(BF16)


def signed_lanes(width):
    lane = lax.broadcasted_iota(jnp.int32, (1, width), 1)
    return jnp.where(lane >= width // 2, lane - width, lane).astype(F32)


def kernel(
    dims,
    exp_hbm,
    inv_hbm,
    val_hbm,
    cor_hbm,
    off_hbm,
    sub_hbm,
    psf_hbm,
    matched_ref,
    weight_ref,
    exp_ref,
    inv_ref,
    val_ref,
    cor_ref,
    off_ref,
    sub_ref,
    psf_ref,
    tile,
    dec_out,
    dec_in,
    mid_out,
    mid_in,
    edge_out,
    edge_in,
    taps,
    bands,
    coadd,
    shifts,
    small_sem,
    load_sem,
    dec_send,
    dec_recv,
    mid_send,
    mid_recv,
    edge_send,
    edge_recv,
):
    epochs, prows, pcols, n_ra, n_dec = dims
    rows, cols = prows - 2 * MARGIN, pcols - 2 * MARGIN
    me_ra, me_dec = lax.axis_index("ra"), lax.axis_index("dec")
    prev_ra, next_ra = lax.rem(me_ra + n_ra - 1, n_ra), lax.rem(me_ra + 1, n_ra)
    has_prev, has_next = me_dec > 0, me_dec < n_dec - 1

    small = [
        pltpu.make_async_copy(src, dst, small_sem.at[i])
        for i, (src, dst) in enumerate(
            ((off_hbm, off_ref), (sub_hbm, sub_ref), (cor_hbm, cor_ref), (psf_hbm, psf_ref))
        )
    ]
    loads = []
    for e in range(epochs):
        for which, (src, dst) in enumerate(
            ((inv_hbm, inv_ref), (val_hbm, val_ref), (exp_hbm, exp_ref))
        ):
            loads.append(pltpu.make_async_copy(src.at[e], dst.at[e], load_sem.at[3 * e + which]))
    for copy in small + loads:
        copy.start()

    barrier = pltpu.get_barrier_semaphore()
    for peer in (prev_ra, next_ra):
        pl.semaphore_signal(barrier, inc=1, device_id=(peer, me_dec), device_id_type=MESH)

    @pl.when(has_prev)
    def _():
        pl.semaphore_signal(barrier, inc=1, device_id=(me_ra, me_dec - 1), device_id_type=MESH)

    @pl.when(has_next)
    def _():
        pl.semaphore_signal(barrier, inc=1, device_id=(me_ra, me_dec + 1), device_id_type=MESH)

    for copy in small[:3]:
        copy.wait()
    inner = prows - 2 * BAND
    side = 2 * LANES
    start = (prows - side) // 2
    row_maps, col_maps = [], []
    for e in range(epochs):
        lanes = signed_lanes(512)
        shift_r = off_ref[0, 0, e, 0].astype(F32) + sub_ref[0, 0, e, 0]
        shift_c = off_ref[0, 0, e, 1].astype(F32) + sub_ref[0, 0, e, 1]
        row = lanczos(shift_r - lanes)
        col = lanczos(shift_c + lanes)
        top = jnp.concatenate(halves(skewed(row, BAND, LANES, 0)), axis=1)
        bottom = jnp.concatenate(halves(skewed(row, BAND, LANES, LANES - BAND)), axis=1)
        middle = jnp.concatenate(halves(skewed(row, inner, side, BAND - start)), axis=0)
        row_maps.append((top, bottom, middle))
        across = halves(skewed(col, pcols, pcols, 0))
        col_maps.append(across)
    spans = ((0, 2 * LANES), (0, pcols), (pcols - 2 * LANES, pcols))
    col_blocks = []
    for block, (first, last) in enumerate(spans):
        picked = slice(block * LANES, (block + 1) * LANES)
        col_blocks.append(
            jnp.concatenate(
                [
                    jnp.concatenate([part[first:last, picked] for part in across], axis=1)
                    for across in col_maps
                ],
                axis=0,
            )
        )

    def column_pass(pieces):
        stacked = [jnp.concatenate([p[:, :pcols], p[:, pcols:]], axis=0) for p in pieces]
        out = []
        for block, (first, last) in enumerate(spans):
            both = dot(jnp.concatenate([p[:, first:last] for p in stacked], axis=1), col_blocks[block])
            out.append(both[:, :LANES] + both[:, LANES:])
        return out

    rim_rows, inner_rows = [], []
    for e in range(epochs):
        for which in range(3):
            loads[3 * e + which].wait()
        top, bottom, middle = row_maps[e]
        masked = inv_ref[e] * val_ref[e].astype(F32) * cor_ref[0, 0, e].astype(F32)
        pixels = jnp.concatenate([(masked * exp_ref[e]).astype(BF16), masked.astype(BF16)], axis=1)
        upper = dot(top, jnp.concatenate([pixels[:LANES]] * 2, axis=0))
        lower = dot(bottom, jnp.concatenate([pixels[prows - LANES :]] * 2, axis=0))
        rim_rows.append(jnp.concatenate([upper.astype(BF16), lower.astype(BF16)], axis=0))
        both = dot(middle, pixels[start : start + side])
        inner_rows.append((both[:inner] + both[inner:]).astype(BF16))

    for block, value in enumerate(column_pass(rim_rows)):
        where = slice(block * LANES, (block + 1) * LANES)
        for plane in range(2):
            for way in range(2):
                part = value[(2 * plane + way) * BAND : (2 * plane + way + 1) * BAND]
                tile[plane, way * (prows - BAND) : way * (prows - BAND) + BAND, where] = part
                dec_out[way, plane, :, where] = part.astype(BF16)
    pl.semaphore_wait(barrier, 2 + has_prev.astype(jnp.int32) + has_next.astype(jnp.int32))

    def dec_copy(way):
        return pltpu.make_async_remote_copy(
            src_ref=dec_out.at[way],
            dst_ref=dec_in.at[way],
            send_sem=dec_send.at[way],
            recv_sem=dec_recv.at[way],
            device_id=(me_ra, me_dec + (1 if way else -1)),
            device_id_type=MESH,
        )

    def mid_copy(way):
        return pltpu.make_async_remote_copy(
            src_ref=mid_out.at[way],
            dst_ref=mid_in.at[way],
            send_sem=mid_send.at[way],
            recv_sem=mid_recv.at[way],
            device_id=(next_ra if way else prev_ra, me_dec),
            device_id_type=MESH,
        )

    def edge_copy(way, part):
        return pltpu.make_async_remote_copy(
            src_ref=edge_out.at[way, part],
            dst_ref=edge_in.at[way, part],
            send_sem=edge_send.at[way, part],
            recv_sem=edge_recv.at[way, part],
            device_id=(next_ra if way else prev_ra, me_dec),
            device_id_type=MESH,
        )

    @pl.when(has_prev)
    def _():
        dec_copy(0).start()

    @pl.when(has_next)
    def _():
        dec_copy(1).start()

    for block, value in enumerate(column_pass(inner_rows)):
        where = slice(block * LANES, (block + 1) * LANES)
        for plane in range(2):
            tile[plane, BAND : BAND + inner, where] = value[plane * inner : (plane + 1) * inner]

    ends = (slice(0, LANES), slice(pcols - LANES, pcols))
    core = slice(2 * MARGIN, prows - 2 * MARGIN)
    for way in range(2):
        mid_out[way] = tile[:, core, ends[way]].astype(BF16)
    for way in range(2):
        mid_copy(way).start()

    small[3].wait()
    side_k = psf_ref.shape[0]
    taps[...] = jnp.zeros_like(taps)
    taps[0:side_k, 0 : psf_ref.shape[1]] = psf_ref[...].astype(F32)
    offset = MARGIN - HALF

    def build(k, carry):
        for s in range(GROUP // 2):
            for parity in range(2):
                row = taps[pl.ds(k * GROUP + 2 * s + parity, 1), :]
                bands[
                    k, parity * LANES : (parity + 1) * LANES, s * 2 * LANES : (s + 1) * 2 * LANES
                ] = skewed(row, LANES, 2 * LANES, offset).astype(BF16)
        return carry

    lax.fori_loop(0, bands.shape[0], build, 0)

    edges = (
        slice(2 * MARGIN - BAND, 2 * MARGIN),
        slice(prows - 2 * MARGIN, prows - 2 * MARGIN + BAND),
    )
    for part, present in ((0, has_prev), (1, has_next)):

        @pl.when(present)
        def _():
            dec_copy(1 - part).wait_recv()
            tile[:, edges[part], :] += dec_in[1 - part].astype(F32)

        for way in range(2):
            edge_out[way, part] = tile[:, edges[part], ends[way]].astype(BF16)
        for way in range(2):
            edge_copy(way, part).start()

    for way in range(2):
        mid_copy(way).wait_recv()
        tile[:, core, ends[1 - way]] += mid_in[way].astype(F32)
    for part in range(2):
        for way in range(2):
            edge_copy(way, part).wait_recv()
            tile[:, edges[part], ends[1 - way]] += edge_in[way, part].astype(F32)

    weight_ref[...] = tile[1, MARGIN : MARGIN + rows, MARGIN : MARGIN + cols]
    row_id = lax.broadcasted_iota(jnp.int32, (coadd.shape[0], 1), 0) - MARGIN + me_dec * rows
    inside = (row_id >= 0) & (row_id < n_dec * rows)
    coadd[...] = jnp.where(inside, tile[0] / jnp.maximum(tile[1], 1.0), 0.0)
    deep = shifts.shape[1]
    for s in range(GROUP // 2):
        first = offset + 2 * s
        moved = coadd[first : first + deep, :].astype(BF16)
        for block in range(2):
            shifts[block, :, s * 2 * LANES : (s + 1) * 2 * LANES] = moved[
                :, block * LANES : (block + 2) * LANES
            ]

    tall = rows + GROUP
    total = jnp.zeros((2 * tall, 2 * LANES), F32)
    for k in range(bands.shape[0]):
        pieces = shifts[:, k * GROUP : k * GROUP + tall, :].reshape(2 * tall, shifts.shape[2])
        total = total + dot_t(pieces, bands[k])
    for block in range(2):
        even = total[block * tall : block * tall + rows, :LANES]
        odd = total[block * tall : (block + 1) * tall, LANES:][1 : rows + 1]
        matched_ref[:, block * LANES : (block + 1) * LANES] = even + odd

    @pl.when(has_prev)
    def _():
        dec_copy(0).wait_send()

    @pl.when(has_next)
    def _():
        dec_copy(1).wait_send()

    for way in range(2):
        mid_copy(way).wait_send()
        for part in range(2):
            edge_copy(way, part).wait_send()


def solution(mesh):
    n_ra, n_dec = mesh.shape["ra"], mesh.shape["dec"]

    def shards(exposures, inv_variance, pixel_valid, correlation, pixel_offset, subpixel, psf_match):
        epochs, prows, pcols = exposures.shape
        rows, cols = prows - 2 * MARGIN, pcols - 2 * MARGIN
        groups = -(-psf_match.shape[0] // GROUP)
        deep = rows + GROUP * groups
        result = jax.ShapeDtypeStruct((rows, cols), F32)
        hbm = pl.BlockSpec(memory_space=pltpu.HBM)
        vmem = pl.BlockSpec(memory_space=pltpu.VMEM)
        return pl.pallas_call(
            functools.partial(kernel, (epochs, prows, pcols, n_ra, n_dec)),
            out_shape=(result, result),
            in_specs=[hbm] * 7,
            out_specs=(vmem, vmem),
            scratch_shapes=[
                pltpu.VMEM((epochs, prows, pcols), F32),
                pltpu.VMEM((epochs, prows, pcols), F32),
                pltpu.VMEM((epochs, prows, pcols), jnp.int32),
                pltpu.SMEM(correlation.shape, jnp.int32),
                pltpu.SMEM(pixel_offset.shape, jnp.int32),
                pltpu.SMEM(subpixel.shape, F32),
                pltpu.VMEM(psf_match.shape, BF16),
                pltpu.VMEM((2, prows, pcols), F32),
                pltpu.VMEM((2, 2, BAND, pcols), BF16),
                pltpu.VMEM((2, 2, BAND, pcols), BF16),
                pltpu.VMEM((2, 2, prows - 4 * MARGIN, LANES), BF16),
                pltpu.VMEM((2, 2, prows - 4 * MARGIN, LANES), BF16),
                pltpu.VMEM((2, 2, 2, BAND, LANES), BF16),
                pltpu.VMEM((2, 2, 2, BAND, LANES), BF16),
                pltpu.VMEM((groups * GROUP, 2 * LANES), F32),
                pltpu.VMEM((groups, 2 * LANES, GROUP * LANES), BF16),
                pltpu.VMEM((prows, pcols), F32),
                pltpu.VMEM((2, deep, GROUP * LANES), BF16),
                pltpu.SemaphoreType.DMA((4,)),
                pltpu.SemaphoreType.DMA((3 * epochs,)),
                pltpu.SemaphoreType.DMA((2,)),
                pltpu.SemaphoreType.DMA((2,)),
                pltpu.SemaphoreType.DMA((2,)),
                pltpu.SemaphoreType.DMA((2,)),
                pltpu.SemaphoreType.DMA((2, 2)),
                pltpu.SemaphoreType.DMA((2, 2)),
            ],
            compiler_params=pltpu.CompilerParams(
                collective_id=0, has_side_effects=True, vmem_limit_bytes=48 * 1024 * 1024
            ),
            name="coadd",
        )(*[pltpu.with_memory_space_constraint(x, pltpu.HBM) for x in (exposures, inv_variance, pixel_valid, correlation, pixel_offset, subpixel, psf_match)])

    return jax.shard_map(
        shards,
        mesh=mesh,
        in_specs=(
            P(None, "dec", "ra"),
            P(None, "dec", "ra"),
            P(None, "dec", "ra"),
            P("dec", "ra", None),
            P("dec", "ra", None, None),
            P("dec", "ra", None, None),
            P(),
        ),
        out_specs=(P("dec", "ra"), P("dec", "ra")),
        check_vma=False,
    )
```

```python
import functools

import jax
import jax.numpy as jnp
from jax import lax
from jax.experimental import pallas as pl
from jax.experimental.pallas import tpu as pltpu
from jax.sharding import PartitionSpec as P

MARGIN = 64
HALF = 31
LANES = 128
BAND = 96
GROUP = 16
F32 = jnp.float32
BF16 = jnp.bfloat16
MESH = pl.DeviceIdType.MESH


def dot(a, b):
    return jnp.dot(a, b, preferred_element_type=F32)


def dot_t(a, b):
    return lax.dot_general(a, b, (((1,), (1,)), ((), ())), preferred_element_type=F32)


def sinc(x):
    angle = jnp.pi * x
    safe = jnp.where(angle == 0.0, 1.0, angle)
    return jnp.where(angle == 0.0, 1.0, jnp.sin(safe) / safe)


def lanczos(x):
    return jnp.where(jnp.abs(x) < 3.0, sinc(x) * sinc(x / 3.0), 0.0)


def skewed(row, count, width, shift):
    spread = jnp.broadcast_to(row, (count, row.shape[1]))
    return pltpu.roll(spread, shift, 1, stride=1, stride_axis=0)[:, :width]


def halves(value):
    high = value.astype(BF16)
    return high, (value - high.astype(F32)).astype(BF16)


def signed_lanes(width):
    lane = lax.broadcasted_iota(jnp.int32, (1, width), 1)
    return jnp.where(lane >= width // 2, lane - width, lane).astype(F32)


def kernel(
    dims,
    exp_hbm,
    inv_hbm,
    val_hbm,
    cor_hbm,
    off_hbm,
    sub_hbm,
    psf_hbm,
    matched_ref,
    weight_ref,
    exp_ref,
    inv_ref,
    val_ref,
    cor_ref,
    off_ref,
    sub_ref,
    psf_ref,
    tile,
    slab,
    dec_out,
    dec_in,
    dec_core_out,
    dec_core_in,
    mid_out,
    mid_in,
    edge_out,
    edge_in,
    taps,
    bands,
    coadd,
    shifts,
    inner_sum,
    small_sem,
    load_sem,
    dec_send,
    dec_recv,
    dec_core_send,
    dec_core_recv,
    mid_send,
    mid_recv,
    edge_send,
    edge_recv,
):
    epochs, prows, pcols, n_ra, n_dec = dims
    rows, cols = prows - 2 * MARGIN, pcols - 2 * MARGIN
    me_ra, me_dec = lax.axis_index("ra"), lax.axis_index("dec")
    prev_ra, next_ra = lax.rem(me_ra + n_ra - 1, n_ra), lax.rem(me_ra + 1, n_ra)
    has_prev, has_next = me_dec > 0, me_dec < n_dec - 1

    small = [
        pltpu.make_async_copy(src, dst, small_sem.at[i])
        for i, (src, dst) in enumerate(
            ((off_hbm, off_ref), (sub_hbm, sub_ref), (cor_hbm, cor_ref), (psf_hbm, psf_ref))
        )
    ]
    loads = []
    for e in range(epochs):
        for which, (src, dst) in enumerate(
            ((inv_hbm, inv_ref), (val_hbm, val_ref), (exp_hbm, exp_ref))
        ):
            loads.append(pltpu.make_async_copy(src.at[e], dst.at[e], load_sem.at[3 * e + which]))
    for copy in small + loads:
        copy.start()

    barrier = pltpu.get_barrier_semaphore()
    for peer in (prev_ra, next_ra):
        pl.semaphore_signal(barrier, inc=1, device_id=(peer, me_dec), device_id_type=MESH)

    @pl.when(has_prev)
    def _():
        pl.semaphore_signal(barrier, inc=1, device_id=(me_ra, me_dec - 1), device_id_type=MESH)

    @pl.when(has_next)
    def _():
        pl.semaphore_signal(barrier, inc=1, device_id=(me_ra, me_dec + 1), device_id_type=MESH)

    for copy in small[:3]:
        copy.wait()
    inner = prows - 2 * BAND
    side = 2 * LANES
    start = (prows - side) // 2
    row_maps, col_maps = [], []
    for e in range(epochs):
        lanes = signed_lanes(512)
        shift_r = off_ref[0, 0, e, 0].astype(F32) + sub_ref[0, 0, e, 0]
        shift_c = off_ref[0, 0, e, 1].astype(F32) + sub_ref[0, 0, e, 1]
        row = lanczos(shift_r - lanes)
        col = lanczos(shift_c + lanes)
        top = jnp.concatenate(halves(skewed(row, BAND, LANES, 0)), axis=1)
        bottom = jnp.concatenate(halves(skewed(row, BAND, LANES, LANES - BAND)), axis=1)
        middle = jnp.concatenate(halves(skewed(row, inner, side, BAND - start)), axis=0)
        row_maps.append((top, bottom, middle))
        across = halves(skewed(col, pcols, pcols, 0))
        col_maps.append(across)
    spans = ((0, 2 * LANES), (0, pcols), (pcols - 2 * LANES, pcols))
    col_blocks = []
    for block, (first, last) in enumerate(spans):
        picked = slice(block * LANES, (block + 1) * LANES)
        col_blocks.append(
            jnp.concatenate(
                [
                    jnp.concatenate([part[first:last, picked] for part in across], axis=1)
                    for across in col_maps
                ],
                axis=0,
            )
        )

    def column_pass(pieces):
        stacked = [jnp.concatenate([p[:, :pcols], p[:, pcols:]], axis=0) for p in pieces]
        out = []
        for block, (first, last) in enumerate(spans):
            both = dot(jnp.concatenate([p[:, first:last] for p in stacked], axis=1), col_blocks[block])
            out.append(both[:, :LANES] + both[:, LANES:])
        return out

    rim_rows, inner_rows = [], []
    for e in range(epochs):
        for which in range(3):
            loads[3 * e + which].wait()
        top, bottom, middle = row_maps[e]
        masked = inv_ref[e] * val_ref[e].astype(F32) * cor_ref[0, 0, e].astype(F32)
        pixels = jnp.concatenate([(masked * exp_ref[e]).astype(BF16), masked.astype(BF16)], axis=1)
        upper = dot(top, jnp.concatenate([pixels[:LANES]] * 2, axis=0))
        lower = dot(bottom, jnp.concatenate([pixels[prows - LANES :]] * 2, axis=0))
        rim_rows.append(jnp.concatenate([upper.astype(BF16), lower.astype(BF16)], axis=0))
        slab[e] = pixels[start : start + side]

    for block, value in enumerate(column_pass(rim_rows)):
        where = slice(block * LANES, (block + 1) * LANES)
        for plane in range(2):
            for way in range(2):
                part = value[(2 * plane + way) * BAND : (2 * plane + way + 1) * BAND]
                tile[plane, way * (prows - BAND) : way * (prows - BAND) + BAND, where] = part
                if block == 1:
                    dec_core_out[way, plane] = part.astype(BF16)
                else:
                    dec_out[way, plane, :, block // 2 * LANES : (block // 2 + 1) * LANES] = (
                        part.astype(BF16)
                    )
    pl.semaphore_wait(barrier, 2 + has_prev.astype(jnp.int32) + has_next.astype(jnp.int32))

    def dec_copy(way):
        return pltpu.make_async_remote_copy(
            src_ref=dec_out.at[way],
            dst_ref=dec_in.at[way],
            send_sem=dec_send.at[way],
            recv_sem=dec_recv.at[way],
            device_id=(me_ra, me_dec + (1 if way else -1)),
            device_id_type=MESH,
        )

    def dec_core_copy(way):
        return pltpu.make_async_remote_copy(
            src_ref=dec_core_out.at[way],
            dst_ref=dec_core_in.at[way],
            send_sem=dec_core_send.at[way],
            recv_sem=dec_core_recv.at[way],
            device_id=(me_ra, me_dec + (1 if way else -1)),
            device_id_type=MESH,
        )

    def mid_copy(way):
        return pltpu.make_async_remote_copy(
            src_ref=mid_out.at[way],
            dst_ref=mid_in.at[way],
            send_sem=mid_send.at[way],
            recv_sem=mid_recv.at[way],
            device_id=(next_ra if way else prev_ra, me_dec),
            device_id_type=MESH,
        )

    def edge_copy(way, part):
        return pltpu.make_async_remote_copy(
            src_ref=edge_out.at[way, part],
            dst_ref=edge_in.at[way, part],
            send_sem=edge_send.at[way, part],
            recv_sem=edge_recv.at[way, part],
            device_id=(next_ra if way else prev_ra, me_dec),
            device_id_type=MESH,
        )

    @pl.when(has_prev)
    def _():
        dec_copy(0).start()
        dec_core_copy(0).start()

    @pl.when(has_next)
    def _():
        dec_copy(1).start()
        dec_core_copy(1).start()

    for e in range(epochs):
        both = dot(row_maps[e][2], slab[e])
        inner_rows.append((both[:inner] + both[inner:]).astype(BF16))
    for block, value in enumerate(column_pass(inner_rows)):
        where = slice(block * LANES, (block + 1) * LANES)
        for plane in range(2):
            tile[plane, BAND : BAND + inner, where] = value[plane * inner : (plane + 1) * inner]

    ends = (slice(0, LANES), slice(pcols - LANES, pcols))
    core = slice(2 * MARGIN, prows - 2 * MARGIN)
    for way in range(2):
        mid_out[way] = tile[:, core, ends[way]].astype(BF16)
    for way in range(2):
        mid_copy(way).start()

    small[3].wait()
    side_k = psf_ref.shape[0]
    taps[...] = jnp.zeros_like(taps)
    taps[0:side_k, 0 : psf_ref.shape[1]] = psf_ref[...].astype(F32)
    offset = MARGIN - HALF

    def build(k, carry):
        for s in range(GROUP // 2):
            for parity in range(2):
                row = taps[pl.ds(k * GROUP + 2 * s + parity, 1), :]
                matrix = skewed(row, LANES, 2 * LANES, offset).astype(BF16)
                for end in range(2):
                    first = (2 * end + parity) * LANES
                    bands[k, first : first + LANES, s * LANES : (s + 1) * LANES] = matrix[
                        :, (1 - end) * LANES : (2 - end) * LANES
                    ]
        return carry

    lax.fori_loop(0, bands.shape[0], build, 0)

    edges = (
        slice(2 * MARGIN - BAND, 2 * MARGIN),
        slice(prows - 2 * MARGIN, prows - 2 * MARGIN + BAND),
    )
    for part, present in ((0, has_prev), (1, has_next)):

        @pl.when(present)
        def _():
            dec_copy(1 - part).wait_recv()
            for end in range(2):
                tile[:, edges[part], ends[end]] += dec_in[
                    1 - part, :, :, end * LANES : (end + 1) * LANES
                ].astype(F32)

        for way in range(2):
            edge_out[way, part] = tile[:, edges[part], ends[way]].astype(BF16)
        for way in range(2):
            edge_copy(way, part).start()

    row_id = lax.broadcasted_iota(jnp.int32, (prows, 1), 0) - MARGIN + me_dec * rows
    inside = (row_id >= 0) & (row_id < n_dec * rows)
    deep, tall = shifts.shape[1], rows + GROUP

    def match(slot, where, chosen):
        coadd[:, where] = jnp.where(
            inside, tile[0, :, where] / jnp.maximum(tile[1, :, where], 1.0), 0.0
        )
        for s in range(GROUP // 2):
            first = offset + 2 * s
            shifts[slot, :, s * LANES : (s + 1) * LANES] = coadd[
                first : first + deep, where
            ].astype(BF16)
        total = None
        for k in range(bands.shape[0]):
            part = dot_t(shifts[slot, k * GROUP : k * GROUP + tall, :], bands[k, chosen, :])
            total = part if total is None else total + part
        return total

    for part, present in ((0, has_prev), (1, has_next)):

        @pl.when(present)
        def _():
            dec_core_copy(1 - part).wait_recv()
            tile[:, edges[part], LANES : 2 * LANES] += dec_core_in[1 - part].astype(F32)

    inner_sum[...] = match(2, slice(LANES, 2 * LANES), slice(0, 4 * LANES))

    for way in range(2):
        mid_copy(way).wait_recv()
        tile[:, core, ends[1 - way]] += mid_in[way].astype(F32)
    for end in range(2):
        for part in range(2):
            edge_copy(1 - end, part).wait_recv()
            tile[:, edges[part], ends[end]] += edge_in[1 - end, part].astype(F32)
        total = match(end, ends[end], slice((1 - end) * 2 * LANES, (2 - end) * 2 * LANES))
        total = total + inner_sum[:, end * 2 * LANES : (end + 1) * 2 * LANES]
        matched_ref[:, end * LANES : (end + 1) * LANES] = (
            total[:rows, :LANES] + total[1 : rows + 1, LANES:]
        )
    weight_ref[...] = tile[1, MARGIN : MARGIN + rows, MARGIN : MARGIN + cols]

    @pl.when(has_prev)
    def _():
        dec_copy(0).wait_send()
        dec_core_copy(0).wait_send()

    @pl.when(has_next)
    def _():
        dec_copy(1).wait_send()
        dec_core_copy(1).wait_send()

    for way in range(2):
        mid_copy(way).wait_send()
        for part in range(2):
            edge_copy(way, part).wait_send()


def finish(matched_in, weight_in, matched_out, weight_out, sems):
    copies = [
        pltpu.make_async_copy(matched_in, matched_out, sems.at[0]),
        pltpu.make_async_copy(weight_in, weight_out, sems.at[1]),
    ]
    for copy in copies:
        copy.start()
    for copy in copies:
        copy.wait()


def solution(mesh):
    n_ra, n_dec = mesh.shape["ra"], mesh.shape["dec"]

    def shards(exposures, inv_variance, pixel_valid, correlation, pixel_offset, subpixel, psf_match):
        epochs, prows, pcols = exposures.shape
        rows, cols = prows - 2 * MARGIN, pcols - 2 * MARGIN
        groups = -(-psf_match.shape[0] // GROUP)
        deep = rows + GROUP * groups
        result = jax.ShapeDtypeStruct((rows, cols), F32)
        hbm = pl.BlockSpec(memory_space=pltpu.HBM)
        vmem = pl.BlockSpec(memory_space=pltpu.VMEM)
        sums = pl.pallas_call(
            functools.partial(kernel, (epochs, prows, pcols, n_ra, n_dec)),
            out_shape=(result, result),
            in_specs=[hbm] * 7,
            out_specs=(vmem, vmem),
            scratch_shapes=[
                pltpu.VMEM((epochs, prows, pcols), F32),
                pltpu.VMEM((epochs, prows, pcols), F32),
                pltpu.VMEM((epochs, prows, pcols), jnp.int32),
                pltpu.SMEM(correlation.shape, jnp.int32),
                pltpu.SMEM(pixel_offset.shape, jnp.int32),
                pltpu.SMEM(subpixel.shape, F32),
                pltpu.VMEM(psf_match.shape, BF16),
                pltpu.VMEM((2, prows, pcols), F32),
                pltpu.VMEM((epochs, 2 * LANES, 2 * pcols), BF16),
                pltpu.VMEM((2, 2, BAND, 2 * LANES), BF16),
                pltpu.VMEM((2, 2, BAND, 2 * LANES), BF16),
                pltpu.VMEM((2, 2, BAND, LANES), BF16),
                pltpu.VMEM((2, 2, BAND, LANES), BF16),
                pltpu.VMEM((2, 2, prows - 4 * MARGIN, LANES), BF16),
                pltpu.VMEM((2, 2, prows - 4 * MARGIN, LANES), BF16),
                pltpu.VMEM((2, 2, 2, BAND, LANES), BF16),
                pltpu.VMEM((2, 2, 2, BAND, LANES), BF16),
                pltpu.VMEM((groups * GROUP, 2 * LANES), F32),
                pltpu.VMEM((groups, 4 * LANES, GROUP // 2 * LANES), BF16),
                pltpu.VMEM((prows, pcols), F32),
                pltpu.VMEM((3, deep, GROUP // 2 * LANES), BF16),
                pltpu.VMEM((rows + GROUP, 4 * LANES), F32),
                pltpu.SemaphoreType.DMA((4,)),
                pltpu.SemaphoreType.DMA((3 * epochs,)),
                pltpu.SemaphoreType.DMA((2,)),
                pltpu.SemaphoreType.DMA((2,)),
                pltpu.SemaphoreType.DMA((2,)),
                pltpu.SemaphoreType.DMA((2,)),
                pltpu.SemaphoreType.DMA((2,)),
                pltpu.SemaphoreType.DMA((2,)),
                pltpu.SemaphoreType.DMA((2, 2)),
                pltpu.SemaphoreType.DMA((2, 2)),
            ],
            compiler_params=pltpu.CompilerParams(
                collective_id=0, has_side_effects=True, vmem_limit_bytes=48 * 1024 * 1024
            ),
            name="coadd",
        )(*[pltpu.with_memory_space_constraint(x, pltpu.HBM) for x in (exposures, inv_variance, pixel_valid, correlation, pixel_offset, subpixel, psf_match)])
        return pl.pallas_call(
            finish,
            out_shape=(result, result),
            in_specs=[vmem, vmem],
            out_specs=(hbm, hbm),
            scratch_shapes=[pltpu.SemaphoreType.DMA((2,))],
            compiler_params=pltpu.CompilerParams(vmem_limit_bytes=1024 * 1024),
            name="finish",
        )(*sums)

    return jax.shard_map(
        shards,
        mesh=mesh,
        in_specs=(
            P(None, "dec", "ra"),
            P(None, "dec", "ra"),
            P(None, "dec", "ra"),
            P("dec", "ra", None),
            P("dec", "ra", None, None),
            P("dec", "ra", None, None),
            P(),
        ),
        out_specs=(P("dec", "ra"), P("dec", "ra")),
        check_vma=False,
    )
```

```python
import functools

import jax
import jax.numpy as jnp
from jax import lax
from jax.experimental import pallas as pl
from jax.experimental.pallas import tpu as pltpu
from jax.sharding import PartitionSpec as P

MARGIN = 64
HALF = 31
LANES = 128
BAND = 96
GROUP = 16
F32 = jnp.float32
BF16 = jnp.bfloat16
MESH = pl.DeviceIdType.MESH


def dot(a, b):
    return jnp.dot(a, b, preferred_element_type=F32)


def dot_t(a, b):
    return lax.dot_general(a, b, (((1,), (1,)), ((), ())), preferred_element_type=F32)


def sinc(x):
    angle = jnp.pi * x
    safe = jnp.where(angle == 0.0, 1.0, angle)
    return jnp.where(angle == 0.0, 1.0, jnp.sin(safe) / safe)


def lanczos(x):
    return jnp.where(jnp.abs(x) < 3.0, sinc(x) * sinc(x / 3.0), 0.0)


def skewed(row, count, width, shift):
    spread = jnp.broadcast_to(row, (count, row.shape[1]))
    return pltpu.roll(spread, shift, 1, stride=1, stride_axis=0)[:, :width]


def halves(value):
    high = value.astype(BF16)
    return high, (value - high.astype(F32)).astype(BF16)


def lane_ids(value):
    return lax.broadcasted_iota(jnp.int32, value.shape, 1)


def packed(planes, way):
    first, second = planes[0], planes[1]
    if way:
        first, second = pltpu.roll(first, BAND, 1), pltpu.roll(second, BAND, 1)
    half = first.shape[0] // 2
    upper = jnp.where(lane_ids(first) < BAND, first, pltpu.roll(second, LANES - BAND, 1))
    low, high = second[:half], second[half:]
    lower = jnp.where(lane_ids(low) < LANES // 2, low, pltpu.roll(high, LANES // 2, 1))
    return jnp.concatenate([upper, lower], axis=0).astype(BF16)


def unpacked(value, way):
    value = value.astype(F32)
    half = value.shape[0] // 3
    upper, lower = value[: 2 * half], value[2 * half :]
    lanes = lane_ids(upper)
    first = jnp.where(lanes < BAND, upper, 0.0)
    low = jnp.concatenate([lower, pltpu.roll(lower, LANES // 2, 1)], axis=0)
    high = jnp.where(lanes < BAND, pltpu.roll(upper, BAND, 1), 0.0)
    second = jnp.where(lanes < LANES // 2, low, high)
    if way:
        first, second = pltpu.roll(first, LANES - BAND, 1), pltpu.roll(second, LANES - BAND, 1)
    return first, second


def signed_lanes(width):
    lane = lax.broadcasted_iota(jnp.int32, (1, width), 1)
    return jnp.where(lane >= width // 2, lane - width, lane).astype(F32)


def kernel(
    dims,
    exp_hbm,
    inv_hbm,
    val_hbm,
    cor_hbm,
    off_hbm,
    sub_hbm,
    psf_hbm,
    matched_ref,
    weight_ref,
    exp_ref,
    inv_ref,
    val_ref,
    cor_ref,
    off_ref,
    sub_ref,
    psf_ref,
    tile,
    slab,
    dec_out,
    dec_in,
    dec_core_out,
    dec_core_in,
    mid_out,
    mid_in,
    edge_out,
    edge_in,
    taps,
    bands,
    coadd,
    shifts,
    inner_sum,
    small_sem,
    load_sem,
    dec_send,
    dec_recv,
    dec_core_send,
    dec_core_recv,
    mid_send,
    mid_recv,
    edge_send,
    edge_recv,
):
    epochs, prows, pcols, n_ra, n_dec = dims
    rows, cols = prows - 2 * MARGIN, pcols - 2 * MARGIN
    me_ra, me_dec = lax.axis_index("ra"), lax.axis_index("dec")
    prev_ra, next_ra = lax.rem(me_ra + n_ra - 1, n_ra), lax.rem(me_ra + 1, n_ra)
    has_prev, has_next = me_dec > 0, me_dec < n_dec - 1

    small = [
        pltpu.make_async_copy(src, dst, small_sem.at[i])
        for i, (src, dst) in enumerate(
            ((off_hbm, off_ref), (sub_hbm, sub_ref), (cor_hbm, cor_ref), (psf_hbm, psf_ref))
        )
    ]
    segments = (
        slice(0, LANES),
        slice(prows - LANES, prows),
        slice(LANES, prows - LANES),
    )

    def load(e, segment, which):
        src, dst = ((inv_hbm, inv_ref), (val_hbm, val_ref), (exp_hbm, exp_ref))[which]
        return pltpu.make_async_copy(
            src.at[e, segments[segment]], dst.at[e, segments[segment]], load_sem.at[e, segment, which]
        )

    order = [(e, segment) for e in range(epochs) for segment in range(2)]
    order += [(e, 2) for e in range(epochs)]
    loads = [load(e, segment, which) for e, segment in order for which in range(3)]
    for copy in small + loads:
        copy.start()

    barrier = pltpu.get_barrier_semaphore()
    for peer in (prev_ra, next_ra):
        pl.semaphore_signal(barrier, inc=1, device_id=(peer, me_dec), device_id_type=MESH)

    @pl.when(has_prev)
    def _():
        pl.semaphore_signal(barrier, inc=1, device_id=(me_ra, me_dec - 1), device_id_type=MESH)

    @pl.when(has_next)
    def _():
        pl.semaphore_signal(barrier, inc=1, device_id=(me_ra, me_dec + 1), device_id_type=MESH)

    for copy in small[:3]:
        copy.wait()
    inner = prows - 2 * BAND
    side = 2 * LANES
    start = (prows - side) // 2
    row_maps, col_maps = [], []
    for e in range(epochs):
        lanes = signed_lanes(512)
        shift_r = off_ref[0, 0, e, 0].astype(F32) + sub_ref[0, 0, e, 0]
        shift_c = off_ref[0, 0, e, 1].astype(F32) + sub_ref[0, 0, e, 1]
        row = lanczos(shift_r - lanes)
        col = lanczos(shift_c + lanes)
        top = jnp.concatenate(halves(skewed(row, BAND, LANES, 0)), axis=1)
        bottom = jnp.concatenate(halves(skewed(row, BAND, LANES, LANES - BAND)), axis=1)
        middle = jnp.concatenate(halves(skewed(row, inner, side, BAND - start)), axis=0)
        row_maps.append((top, bottom, middle))
        across = halves(skewed(col, pcols, pcols, 0))
        col_maps.append(across)
    spans = ((0, 2 * LANES), (0, pcols), (pcols - 2 * LANES, pcols))
    col_blocks = []
    for block, (first, last) in enumerate(spans):
        picked = slice(block * LANES, (block + 1) * LANES)
        col_blocks.append(
            jnp.concatenate(
                [
                    jnp.concatenate([part[first:last, picked] for part in across], axis=1)
                    for across in col_maps
                ],
                axis=0,
            )
        )

    def column_pass(pieces):
        stacked = [jnp.concatenate([p[:, :pcols], p[:, pcols:]], axis=0) for p in pieces]
        out = []
        for block, (first, last) in enumerate(spans):
            both = dot(jnp.concatenate([p[:, first:last] for p in stacked], axis=1), col_blocks[block])
            out.append(both[:, :LANES] + both[:, LANES:])
        return out

    rim_rows, inner_rows = [], []
    def pixels(e, segment):
        for which in range(3):
            load(e, segment, which).wait()
        at = segments[segment]
        masked = inv_ref[e, at] * val_ref[e, at].astype(F32) * cor_ref[0, 0, e].astype(F32)
        return jnp.concatenate([(masked * exp_ref[e, at]).astype(BF16), masked.astype(BF16)], axis=1)

    reach = LANES - start
    for e in range(epochs):
        rims = []
        for segment in range(2):
            part = pixels(e, segment)
            rims.append(
                dot(row_maps[e][segment], jnp.concatenate([part, part], axis=0)).astype(BF16)
            )
            if segment:
                slab[e, side - reach : side] = part[:reach]
            else:
                slab[e, 0:reach] = part[start:]
        rim_rows.append(jnp.concatenate(rims, axis=0))

    for block, value in enumerate(column_pass(rim_rows)):
        where = slice(block * LANES, (block + 1) * LANES)
        for plane in range(2):
            for way in range(2):
                part = value[(2 * plane + way) * BAND : (2 * plane + way + 1) * BAND]
                tile[plane, way * (prows - BAND) : way * (prows - BAND) + BAND, where] = part
                if block == 1:
                    dec_core_out[way, plane] = part.astype(BF16)
                else:
                    dec_out[way, plane, :, block // 2 * LANES : (block // 2 + 1) * LANES] = (
                        part.astype(BF16)
                    )
    pl.semaphore_wait(barrier, 2 + has_prev.astype(jnp.int32) + has_next.astype(jnp.int32))

    def dec_copy(way):
        return pltpu.make_async_remote_copy(
            src_ref=dec_out.at[way],
            dst_ref=dec_in.at[way],
            send_sem=dec_send.at[way],
            recv_sem=dec_recv.at[way],
            device_id=(me_ra, me_dec + (1 if way else -1)),
            device_id_type=MESH,
        )

    def dec_core_copy(way):
        return pltpu.make_async_remote_copy(
            src_ref=dec_core_out.at[way],
            dst_ref=dec_core_in.at[way],
            send_sem=dec_core_send.at[way],
            recv_sem=dec_core_recv.at[way],
            device_id=(me_ra, me_dec + (1 if way else -1)),
            device_id_type=MESH,
        )

    def mid_copy(way):
        return pltpu.make_async_remote_copy(
            src_ref=mid_out.at[way],
            dst_ref=mid_in.at[way],
            send_sem=mid_send.at[way],
            recv_sem=mid_recv.at[way],
            device_id=(next_ra if way else prev_ra, me_dec),
            device_id_type=MESH,
        )

    def edge_copy(way, part):
        return pltpu.make_async_remote_copy(
            src_ref=edge_out.at[way, part],
            dst_ref=edge_in.at[way, part],
            send_sem=edge_send.at[way, part],
            recv_sem=edge_recv.at[way, part],
            device_id=(next_ra if way else prev_ra, me_dec),
            device_id_type=MESH,
        )

    @pl.when(has_prev)
    def _():
        dec_copy(0).start()
        dec_core_copy(0).start()

    @pl.when(has_next)
    def _():
        dec_copy(1).start()
        dec_core_copy(1).start()

    for e in range(epochs):
        slab[e, reach : side - reach] = pixels(e, 2)
        both = dot(row_maps[e][2], slab[e])
        inner_rows.append((both[:inner] + both[inner:]).astype(BF16))
    for block, value in enumerate(column_pass(inner_rows)):
        where = slice(block * LANES, (block + 1) * LANES)
        for plane in range(2):
            tile[plane, BAND : BAND + inner, where] = value[plane * inner : (plane + 1) * inner]

    ends = (slice(0, LANES), slice(pcols - LANES, pcols))
    core = slice(2 * MARGIN, prows - 2 * MARGIN)
    for way in range(2):
        mid_out[way] = packed(tile[:, core, ends[way]], way)
    for way in range(2):
        mid_copy(way).start()

    small[3].wait()
    side_k = psf_ref.shape[0]
    taps[...] = jnp.zeros_like(taps)
    taps[0:side_k, 0 : psf_ref.shape[1]] = psf_ref[...].astype(F32)
    offset = MARGIN - HALF

    def build(k, carry):
        for s in range(GROUP // 2):
            for parity in range(2):
                row = taps[pl.ds(k * GROUP + 2 * s + parity, 1), :]
                matrix = skewed(row, LANES, 2 * LANES, offset).astype(BF16)
                for end in range(2):
                    first = (2 * end + parity) * LANES
                    bands[k, first : first + LANES, s * LANES : (s + 1) * LANES] = matrix[
                        :, (1 - end) * LANES : (2 - end) * LANES
                    ]
        return carry

    lax.fori_loop(0, bands.shape[0], build, 0)

    edges = (
        slice(2 * MARGIN - BAND, 2 * MARGIN),
        slice(prows - 2 * MARGIN, prows - 2 * MARGIN + BAND),
    )
    for part, present in ((0, has_prev), (1, has_next)):

        @pl.when(present)
        def _():
            dec_copy(1 - part).wait_recv()
            for end in range(2):
                tile[:, edges[part], ends[end]] += dec_in[
                    1 - part, :, :, end * LANES : (end + 1) * LANES
                ].astype(F32)

        for way in range(2):
            edge_out[way, part] = packed(tile[:, edges[part], ends[way]], way)
        for way in range(2):
            edge_copy(way, part).start()

    row_id = lax.broadcasted_iota(jnp.int32, (prows, 1), 0) - MARGIN + me_dec * rows
    inside = (row_id >= 0) & (row_id < n_dec * rows)
    deep, tall = shifts.shape[1], rows + GROUP

    def spread(slot, where):
        coadd[:, where] = jnp.where(
            inside, tile[0, :, where] / jnp.maximum(tile[1, :, where], 1.0), 0.0
        )
        for s in range(GROUP // 2):
            first = offset + 2 * s
            shifts[slot, :, s * LANES : (s + 1) * LANES] = coadd[
                first : first + deep, where
            ].astype(BF16)

    def product(slot, k, chosen):
        return dot_t(shifts[slot, k * GROUP : k * GROUP + tall, :], bands[k, chosen, :])

    for part, present in ((0, has_prev), (1, has_next)):

        @pl.when(present)
        def _():
            dec_core_copy(1 - part).wait_recv()
            tile[:, edges[part], LANES : 2 * LANES] += dec_core_in[1 - part].astype(F32)

    spread(2, slice(LANES, 2 * LANES))
    total = product(2, 0, slice(None))
    for k in range(1, bands.shape[0]):
        total = total + product(2, k, slice(None))
    inner_sum[...] = total

    for way in range(2):
        mid_copy(way).wait_recv()
        for plane, part in enumerate(unpacked(mid_in[way], way)):
            tile[plane, core, ends[1 - way]] += part
    for part in range(2):
        for way in range(2):
            edge_copy(way, part).wait_recv()
            for plane, value in enumerate(unpacked(edge_in[way, part], way)):
                tile[plane, edges[part], ends[1 - way]] += value
    for end in range(2):
        spread(end, ends[end])
    totals = [
        inner_sum[:, end * 2 * LANES : (end + 1) * 2 * LANES] for end in range(2)
    ]
    for k in range(bands.shape[0]):
        for end in range(2):
            totals[end] = totals[end] + product(
                end, k, slice((1 - end) * 2 * LANES, (2 - end) * 2 * LANES)
            )
    for end in range(2):
        matched_ref[:, end * LANES : (end + 1) * LANES] = (
            totals[end][:rows, :LANES] + totals[end][1 : rows + 1, LANES:]
        )
    weight_ref[...] = tile[1, MARGIN : MARGIN + rows, MARGIN : MARGIN + cols]

    @pl.when(has_prev)
    def _():
        dec_copy(0).wait_send()
        dec_core_copy(0).wait_send()

    @pl.when(has_next)
    def _():
        dec_copy(1).wait_send()
        dec_core_copy(1).wait_send()

    for way in range(2):
        mid_copy(way).wait_send()
        for part in range(2):
            edge_copy(way, part).wait_send()


def finish(matched_in, weight_in, matched_out, weight_out, sems):
    copies = [
        pltpu.make_async_copy(matched_in, matched_out, sems.at[0]),
        pltpu.make_async_copy(weight_in, weight_out, sems.at[1]),
    ]
    for copy in copies:
        copy.start()
    for copy in copies:
        copy.wait()


def solution(mesh):
    n_ra, n_dec = mesh.shape["ra"], mesh.shape["dec"]

    def shards(exposures, inv_variance, pixel_valid, correlation, pixel_offset, subpixel, psf_match):
        epochs, prows, pcols = exposures.shape
        rows, cols = prows - 2 * MARGIN, pcols - 2 * MARGIN
        groups = -(-psf_match.shape[0] // GROUP)
        deep = rows + GROUP * groups
        result = jax.ShapeDtypeStruct((rows, cols), F32)
        hbm = pl.BlockSpec(memory_space=pltpu.HBM)
        vmem = pl.BlockSpec(memory_space=pltpu.VMEM)
        sums = pl.pallas_call(
            functools.partial(kernel, (epochs, prows, pcols, n_ra, n_dec)),
            out_shape=(result, result),
            in_specs=[hbm] * 7,
            out_specs=(vmem, vmem),
            scratch_shapes=[
                pltpu.VMEM((epochs, prows, pcols), F32),
                pltpu.VMEM((epochs, prows, pcols), F32),
                pltpu.VMEM((epochs, prows, pcols), jnp.int32),
                pltpu.SMEM(correlation.shape, jnp.int32),
                pltpu.SMEM(pixel_offset.shape, jnp.int32),
                pltpu.SMEM(subpixel.shape, F32),
                pltpu.VMEM(psf_match.shape, BF16),
                pltpu.VMEM((2, prows, pcols), F32),
                pltpu.VMEM((epochs, 2 * LANES, 2 * pcols), BF16),
                pltpu.VMEM((2, 2, BAND, 2 * LANES), BF16),
                pltpu.VMEM((2, 2, BAND, 2 * LANES), BF16),
                pltpu.VMEM((2, 2, BAND, LANES), BF16),
                pltpu.VMEM((2, 2, BAND, LANES), BF16),
                pltpu.VMEM((2, (prows - 4 * MARGIN) * 3 // 2, LANES), BF16),
                pltpu.VMEM((2, (prows - 4 * MARGIN) * 3 // 2, LANES), BF16),
                pltpu.VMEM((2, 2, BAND * 3 // 2, LANES), BF16),
                pltpu.VMEM((2, 2, BAND * 3 // 2, LANES), BF16),
                pltpu.VMEM((groups * GROUP, 2 * LANES), F32),
                pltpu.VMEM((groups, 4 * LANES, GROUP // 2 * LANES), BF16),
                pltpu.VMEM((prows, pcols), F32),
                pltpu.VMEM((3, deep, GROUP // 2 * LANES), BF16),
                pltpu.VMEM((rows + GROUP, 4 * LANES), F32),
                pltpu.SemaphoreType.DMA((4,)),
                pltpu.SemaphoreType.DMA((epochs, 3, 3)),
                pltpu.SemaphoreType.DMA((2,)),
                pltpu.SemaphoreType.DMA((2,)),
                pltpu.SemaphoreType.DMA((2,)),
                pltpu.SemaphoreType.DMA((2,)),
                pltpu.SemaphoreType.DMA((2,)),
                pltpu.SemaphoreType.DMA((2,)),
                pltpu.SemaphoreType.DMA((2, 2)),
                pltpu.SemaphoreType.DMA((2, 2)),
            ],
            compiler_params=pltpu.CompilerParams(
                collective_id=0, has_side_effects=True, vmem_limit_bytes=48 * 1024 * 1024
            ),
            name="coadd",
        )(*[pltpu.with_memory_space_constraint(x, pltpu.HBM) for x in (exposures, inv_variance, pixel_valid, correlation, pixel_offset, subpixel, psf_match)])
        return pl.pallas_call(
            finish,
            out_shape=(result, result),
            in_specs=[vmem, vmem],
            out_specs=(hbm, hbm),
            scratch_shapes=[pltpu.SemaphoreType.DMA((2,))],
            compiler_params=pltpu.CompilerParams(vmem_limit_bytes=1024 * 1024),
            name="finish",
        )(*sums)

    return jax.shard_map(
        shards,
        mesh=mesh,
        in_specs=(
            P(None, "dec", "ra"),
            P(None, "dec", "ra"),
            P(None, "dec", "ra"),
            P("dec", "ra", None),
            P("dec", "ra", None, None),
            P("dec", "ra", None, None),
            P(),
        ),
        out_specs=(P("dec", "ra"), P("dec", "ra")),
        check_vma=False,
    )
```

```python
import functools

import jax
import jax.numpy as jnp
from jax import lax
from jax.experimental import pallas as pl
from jax.experimental.pallas import tpu as pltpu
from jax.sharding import PartitionSpec as P

MARGIN = 64
HALF = 31
LANES = 128
BAND = 96
GROUP = 16
F32 = jnp.float32
BF16 = jnp.bfloat16
MESH = pl.DeviceIdType.MESH


def dot(a, b):
    return jnp.dot(a, b, preferred_element_type=F32)


def dot_t(a, b):
    return lax.dot_general(a, b, (((1,), (1,)), ((), ())), preferred_element_type=F32)


def sinc(x):
    angle = jnp.pi * x
    safe = jnp.where(angle == 0.0, 1.0, angle)
    return jnp.where(angle == 0.0, 1.0, jnp.sin(safe) / safe)


def lanczos(x):
    return jnp.where(jnp.abs(x) < 3.0, sinc(x) * sinc(x / 3.0), 0.0)


def skewed(row, count, width, shift):
    spread = jnp.broadcast_to(row, (count, row.shape[1]))
    return pltpu.roll(spread, shift, 1, stride=1, stride_axis=0)[:, :width]


def halves(value):
    high = value.astype(BF16)
    return high, (value - high.astype(F32)).astype(BF16)


def lane_ids(value):
    return lax.broadcasted_iota(jnp.int32, value.shape, 1)


def packed(planes, way):
    first, second = planes[0], planes[1]
    if way:
        first, second = pltpu.roll(first, BAND, 1), pltpu.roll(second, BAND, 1)
    half = first.shape[0] // 2
    upper = jnp.where(lane_ids(first) < BAND, first, pltpu.roll(second, LANES - BAND, 1))
    low, high = second[:half], second[half:]
    lower = jnp.where(lane_ids(low) < LANES // 2, low, pltpu.roll(high, LANES // 2, 1))
    return jnp.concatenate([upper, lower], axis=0).astype(BF16)


def unpacked(value, way):
    value = value.astype(F32)
    half = value.shape[0] // 3
    upper, lower = value[: 2 * half], value[2 * half :]
    lanes = lane_ids(upper)
    first = jnp.where(lanes < BAND, upper, 0.0)
    low = jnp.concatenate([lower, pltpu.roll(lower, LANES // 2, 1)], axis=0)
    high = jnp.where(lanes < BAND, pltpu.roll(upper, BAND, 1), 0.0)
    second = jnp.where(lanes < LANES // 2, low, high)
    if way:
        first, second = pltpu.roll(first, LANES - BAND, 1), pltpu.roll(second, LANES - BAND, 1)
    return first, second


def signed_lanes(width):
    lane = lax.broadcasted_iota(jnp.int32, (1, width), 1)
    return jnp.where(lane >= width // 2, lane - width, lane).astype(F32)


def kernel(
    dims,
    exp_hbm,
    inv_hbm,
    val_hbm,
    cor_hbm,
    off_hbm,
    sub_hbm,
    psf_hbm,
    matched_ref,
    weight_ref,
    exp_ref,
    inv_ref,
    val_ref,
    cor_ref,
    off_ref,
    sub_ref,
    psf_ref,
    tile,
    slab,
    dec_out,
    dec_in,
    dec_core_out,
    dec_core_in,
    mid_out,
    mid_in,
    edge_out,
    edge_in,
    taps,
    bands,
    coadd,
    shifts,
    inner_sum,
    small_sem,
    load_sem,
    dec_send,
    dec_recv,
    dec_core_send,
    dec_core_recv,
    mid_send,
    mid_recv,
    edge_send,
    edge_recv,
):
    epochs, prows, pcols, n_ra, n_dec = dims
    rows, cols = prows - 2 * MARGIN, pcols - 2 * MARGIN
    me_ra, me_dec = lax.axis_index("ra"), lax.axis_index("dec")
    prev_ra, next_ra = lax.rem(me_ra + n_ra - 1, n_ra), lax.rem(me_ra + 1, n_ra)
    has_prev, has_next = me_dec > 0, me_dec < n_dec - 1

    small = [
        pltpu.make_async_copy(src, dst, small_sem.at[i])
        for i, (src, dst) in enumerate(
            ((off_hbm, off_ref), (sub_hbm, sub_ref), (cor_hbm, cor_ref), (psf_hbm, psf_ref))
        )
    ]
    segments = (
        slice(0, LANES),
        slice(prows - LANES, prows),
        slice(LANES, prows - LANES),
    )

    def load(e, segment, which):
        src, dst = ((inv_hbm, inv_ref), (val_hbm, val_ref), (exp_hbm, exp_ref))[which]
        return pltpu.make_async_copy(
            src.at[e, segments[segment]], dst.at[e, segments[segment]], load_sem.at[e, segment, which]
        )

    order = [(e, segment) for e in range(epochs) for segment in range(2)]
    order += [(e, 2) for e in range(epochs)]
    loads = [load(e, segment, which) for e, segment in order for which in range(3)]
    for copy in small + loads:
        copy.start()

    barrier = pltpu.get_barrier_semaphore()
    for peer in (prev_ra, next_ra):
        pl.semaphore_signal(barrier, inc=1, device_id=(peer, me_dec), device_id_type=MESH)

    @pl.when(has_prev)
    def _():
        pl.semaphore_signal(barrier, inc=1, device_id=(me_ra, me_dec - 1), device_id_type=MESH)

    @pl.when(has_next)
    def _():
        pl.semaphore_signal(barrier, inc=1, device_id=(me_ra, me_dec + 1), device_id_type=MESH)

    for copy in small[:3]:
        copy.wait()
    inner = prows - 2 * BAND
    side = 2 * LANES
    start = (prows - side) // 2
    row_maps, col_maps = [], []
    for e in range(epochs):
        lanes = signed_lanes(512)
        shift_r = off_ref[0, 0, e, 0].astype(F32) + sub_ref[0, 0, e, 0]
        shift_c = off_ref[0, 0, e, 1].astype(F32) + sub_ref[0, 0, e, 1]
        row = lanczos(shift_r - lanes)
        col = lanczos(shift_c + lanes)
        top = jnp.concatenate(halves(skewed(row, BAND, LANES, 0)), axis=1)
        bottom = jnp.concatenate(halves(skewed(row, BAND, LANES, LANES - BAND)), axis=1)
        middle = jnp.concatenate(halves(skewed(row, inner, side, BAND - start)), axis=0)
        row_maps.append((top, bottom, middle))
        across = halves(skewed(col, pcols, pcols, 0))
        col_maps.append(across)
    spans = ((0, 2 * LANES), (0, pcols), (pcols - 2 * LANES, pcols))
    col_blocks = []
    for block, (first, last) in enumerate(spans):
        picked = slice(block * LANES, (block + 1) * LANES)
        col_blocks.append(
            jnp.concatenate(
                [
                    jnp.concatenate([part[first:last, picked] for part in across], axis=1)
                    for across in col_maps
                ],
                axis=0,
            )
        )

    def column_pass(pieces):
        stacked = [jnp.concatenate([p[:, :pcols], p[:, pcols:]], axis=0) for p in pieces]
        out = []
        for block, (first, last) in enumerate(spans):
            both = dot(jnp.concatenate([p[:, first:last] for p in stacked], axis=1), col_blocks[block])
            out.append(both[:, :LANES] + both[:, LANES:])
        return out

    rim_rows, inner_rows = [], []
    def pixels(e, segment):
        for which in range(3):
            load(e, segment, which).wait()
        at = segments[segment]
        masked = inv_ref[e, at] * val_ref[e, at].astype(F32) * cor_ref[0, 0, e].astype(F32)
        return jnp.concatenate([(masked * exp_ref[e, at]).astype(BF16), masked.astype(BF16)], axis=1)

    reach = LANES - start
    for e in range(epochs):
        rims = []
        for segment in range(2):
            part = pixels(e, segment)
            rims.append(
                dot(row_maps[e][segment], jnp.concatenate([part, part], axis=0)).astype(BF16)
            )
            if segment:
                slab[e, side - reach : side] = part[:reach]
            else:
                slab[e, 0:reach] = part[start:]
        rim_rows.append(jnp.concatenate(rims, axis=0))

    for block, value in enumerate(column_pass(rim_rows)):
        where = slice(block * LANES, (block + 1) * LANES)
        for plane in range(2):
            for way in range(2):
                part = value[(2 * plane + way) * BAND : (2 * plane + way + 1) * BAND]
                tile[plane, way * (prows - BAND) : way * (prows - BAND) + BAND, where] = part
                if block == 1:
                    dec_core_out[way, plane] = part.astype(BF16)
                else:
                    dec_out[way, plane, :, block // 2 * LANES : (block // 2 + 1) * LANES] = (
                        part.astype(BF16)
                    )
    pl.semaphore_wait(barrier, 2 + has_prev.astype(jnp.int32) + has_next.astype(jnp.int32))

    def dec_copy(way):
        return pltpu.make_async_remote_copy(
            src_ref=dec_out.at[way],
            dst_ref=dec_in.at[way],
            send_sem=dec_send.at[way],
            recv_sem=dec_recv.at[way],
            device_id=(me_ra, me_dec + (1 if way else -1)),
            device_id_type=MESH,
        )

    def dec_core_copy(way):
        return pltpu.make_async_remote_copy(
            src_ref=dec_core_out.at[way],
            dst_ref=dec_core_in.at[way],
            send_sem=dec_core_send.at[way],
            recv_sem=dec_core_recv.at[way],
            device_id=(me_ra, me_dec + (1 if way else -1)),
            device_id_type=MESH,
        )

    def mid_copy(way):
        return pltpu.make_async_remote_copy(
            src_ref=mid_out.at[way],
            dst_ref=mid_in.at[way],
            send_sem=mid_send.at[way],
            recv_sem=mid_recv.at[way],
            device_id=(next_ra if way else prev_ra, me_dec),
            device_id_type=MESH,
        )

    def edge_copy(way, part):
        return pltpu.make_async_remote_copy(
            src_ref=edge_out.at[way, part],
            dst_ref=edge_in.at[way, part],
            send_sem=edge_send.at[way, part],
            recv_sem=edge_recv.at[way, part],
            device_id=(next_ra if way else prev_ra, me_dec),
            device_id_type=MESH,
        )

    @pl.when(has_prev)
    def _():
        dec_copy(0).start()
        dec_core_copy(0).start()

    @pl.when(has_next)
    def _():
        dec_copy(1).start()
        dec_core_copy(1).start()

    for e in range(epochs):
        slab[e, reach : side - reach] = pixels(e, 2)
        both = dot(row_maps[e][2], slab[e])
        inner_rows.append((both[:inner] + both[inner:]).astype(BF16))
    for block, value in enumerate(column_pass(inner_rows)):
        where = slice(block * LANES, (block + 1) * LANES)
        for plane in range(2):
            tile[plane, BAND : BAND + inner, where] = value[plane * inner : (plane + 1) * inner]

    ends = (slice(0, LANES), slice(pcols - LANES, pcols))
    core = slice(2 * MARGIN, prows - 2 * MARGIN)
    for way in range(2):
        mid_out[way] = packed(tile[:, core, ends[way]], way)
    for way in range(2):
        mid_copy(way).start()

    small[3].wait()
    side_k = psf_ref.shape[0]
    taps[...] = jnp.zeros_like(taps)
    taps[0:side_k, 0 : psf_ref.shape[1]] = psf_ref[...].astype(F32)
    offset = MARGIN - HALF

    def build(k, carry):
        for s in range(GROUP // 2):
            for parity in range(2):
                row = taps[pl.ds(k * GROUP + 2 * s + parity, 1), :]
                matrix = skewed(row, LANES, 2 * LANES, offset).astype(BF16)
                for end in range(2):
                    first = (2 * end + parity) * LANES
                    bands[k, first : first + LANES, s * LANES : (s + 1) * LANES] = matrix[
                        :, (1 - end) * LANES : (2 - end) * LANES
                    ]
        return carry

    lax.fori_loop(0, bands.shape[0], build, 0)

    edges = (
        slice(2 * MARGIN - BAND, 2 * MARGIN),
        slice(prows - 2 * MARGIN, prows - 2 * MARGIN + BAND),
    )
    for part, present in ((0, has_prev), (1, has_next)):

        @pl.when(present)
        def _():
            dec_copy(1 - part).wait_recv()
            for end in range(2):
                tile[:, edges[part], ends[end]] += dec_in[
                    1 - part, :, :, end * LANES : (end + 1) * LANES
                ].astype(F32)

        for way in range(2):
            edge_out[way, part] = packed(tile[:, edges[part], ends[way]], way)
        for way in range(2):
            edge_copy(way, part).start()

    span = coadd.shape[0]
    row_id = lax.broadcasted_iota(jnp.int32, (span, 1), 0) - HALF + me_dec * rows
    inside = (row_id >= 0) & (row_id < n_dec * rows)
    deep, tall = shifts.shape[1], rows + GROUP

    def spread(slot, where):
        numer = tile[0, offset : offset + span, where]
        denom = tile[1, offset : offset + span, where]
        coadd[:, where] = jnp.where(inside, numer / jnp.maximum(denom, 1.0), 0.0).astype(BF16)
        for s in range(GROUP // 2):
            shifts[slot, :, s * LANES : (s + 1) * LANES] = coadd[2 * s : 2 * s + deep, where]

    def product(slot, k, chosen):
        return dot_t(shifts[slot, k * GROUP : k * GROUP + tall, :], bands[k, chosen, :])

    for part, present in ((0, has_prev), (1, has_next)):

        @pl.when(present)
        def _():
            dec_core_copy(1 - part).wait_recv()
            tile[:, edges[part], LANES : 2 * LANES] += dec_core_in[1 - part].astype(F32)

    spread(2, slice(LANES, 2 * LANES))
    total = product(2, 0, slice(None))
    for k in range(1, bands.shape[0]):
        total = total + product(2, k, slice(None))
    inner_sum[...] = total

    for way in range(2):
        mid_copy(way).wait_recv()
        for plane, part in enumerate(unpacked(mid_in[way], way)):
            tile[plane, core, ends[1 - way]] += part
    for part in range(2):
        for way in range(2):
            edge_copy(way, part).wait_recv()
            for plane, value in enumerate(unpacked(edge_in[way, part], way)):
                tile[plane, edges[part], ends[1 - way]] += value
    for end in range(2):
        spread(end, ends[end])
    totals = [
        inner_sum[:, end * 2 * LANES : (end + 1) * 2 * LANES] for end in range(2)
    ]
    for k in range(bands.shape[0]):
        for end in range(2):
            totals[end] = totals[end] + product(
                end, k, slice((1 - end) * 2 * LANES, (2 - end) * 2 * LANES)
            )
    for end in range(2):
        matched_ref[:, end * LANES : (end + 1) * LANES] = (
            totals[end][:rows, :LANES] + totals[end][1 : rows + 1, LANES:]
        )
    weight_ref[...] = tile[1, MARGIN : MARGIN + rows, MARGIN : MARGIN + cols]

    @pl.when(has_prev)
    def _():
        dec_copy(0).wait_send()
        dec_core_copy(0).wait_send()

    @pl.when(has_next)
    def _():
        dec_copy(1).wait_send()
        dec_core_copy(1).wait_send()

    for way in range(2):
        mid_copy(way).wait_send()
        for part in range(2):
            edge_copy(way, part).wait_send()


def finish(matched_in, weight_in, matched_out, weight_out, sems):
    copies = [
        pltpu.make_async_copy(matched_in, matched_out, sems.at[0]),
        pltpu.make_async_copy(weight_in, weight_out, sems.at[1]),
    ]
    for copy in copies:
        copy.start()
    for copy in copies:
        copy.wait()


def solution(mesh):
    n_ra, n_dec = mesh.shape["ra"], mesh.shape["dec"]

    def shards(exposures, inv_variance, pixel_valid, correlation, pixel_offset, subpixel, psf_match):
        epochs, prows, pcols = exposures.shape
        rows, cols = prows - 2 * MARGIN, pcols - 2 * MARGIN
        groups = -(-psf_match.shape[0] // GROUP)
        deep = rows + GROUP * groups
        result = jax.ShapeDtypeStruct((rows, cols), F32)
        hbm = pl.BlockSpec(memory_space=pltpu.HBM)
        vmem = pl.BlockSpec(memory_space=pltpu.VMEM)
        sums = pl.pallas_call(
            functools.partial(kernel, (epochs, prows, pcols, n_ra, n_dec)),
            out_shape=(result, result),
            in_specs=[hbm] * 7,
            out_specs=(vmem, vmem),
            scratch_shapes=[
                pltpu.VMEM((epochs, prows, pcols), F32),
                pltpu.VMEM((epochs, prows, pcols), F32),
                pltpu.VMEM((epochs, prows, pcols), jnp.int32),
                pltpu.SMEM(correlation.shape, jnp.int32),
                pltpu.SMEM(pixel_offset.shape, jnp.int32),
                pltpu.SMEM(subpixel.shape, F32),
                pltpu.VMEM(psf_match.shape, BF16),
                pltpu.VMEM((2, prows, pcols), F32),
                pltpu.VMEM((epochs, 2 * LANES, 2 * pcols), BF16),
                pltpu.VMEM((2, 2, BAND, 2 * LANES), BF16),
                pltpu.VMEM((2, 2, BAND, 2 * LANES), BF16),
                pltpu.VMEM((2, 2, BAND, LANES), BF16),
                pltpu.VMEM((2, 2, BAND, LANES), BF16),
                pltpu.VMEM((2, (prows - 4 * MARGIN) * 3 // 2, LANES), BF16),
                pltpu.VMEM((2, (prows - 4 * MARGIN) * 3 // 2, LANES), BF16),
                pltpu.VMEM((2, 2, BAND * 3 // 2, LANES), BF16),
                pltpu.VMEM((2, 2, BAND * 3 // 2, LANES), BF16),
                pltpu.VMEM((groups * GROUP, 2 * LANES), F32),
                pltpu.VMEM((groups, 4 * LANES, GROUP // 2 * LANES), BF16),
                pltpu.VMEM((deep + GROUP, pcols), BF16),
                pltpu.VMEM((3, deep, GROUP // 2 * LANES), BF16),
                pltpu.VMEM((rows + GROUP, 4 * LANES), F32),
                pltpu.SemaphoreType.DMA((4,)),
                pltpu.SemaphoreType.DMA((epochs, 3, 3)),
                pltpu.SemaphoreType.DMA((2,)),
                pltpu.SemaphoreType.DMA((2,)),
                pltpu.SemaphoreType.DMA((2,)),
                pltpu.SemaphoreType.DMA((2,)),
                pltpu.SemaphoreType.DMA((2,)),
                pltpu.SemaphoreType.DMA((2,)),
                pltpu.SemaphoreType.DMA((2, 2)),
                pltpu.SemaphoreType.DMA((2, 2)),
            ],
            compiler_params=pltpu.CompilerParams(
                collective_id=0, has_side_effects=True, vmem_limit_bytes=48 * 1024 * 1024
            ),
            name="coadd",
        )(*[pltpu.with_memory_space_constraint(x, pltpu.HBM) for x in (exposures, inv_variance, pixel_valid, correlation, pixel_offset, subpixel, psf_match)])
        return pl.pallas_call(
            finish,
            out_shape=(result, result),
            in_specs=[vmem, vmem],
            out_specs=(hbm, hbm),
            scratch_shapes=[pltpu.SemaphoreType.DMA((2,))],
            compiler_params=pltpu.CompilerParams(vmem_limit_bytes=1024 * 1024),
            name="finish",
        )(*sums)

    return jax.shard_map(
        shards,
        mesh=mesh,
        in_specs=(
            P(None, "dec", "ra"),
            P(None, "dec", "ra"),
            P(None, "dec", "ra"),
            P("dec", "ra", None),
            P("dec", "ra", None, None),
            P("dec", "ra", None, None),
            P(),
        ),
        out_specs=(P("dec", "ra"), P("dec", "ra")),
        check_vma=False,
    )
```
